32 devices in a mesh: parts: 2 (over x), row: 16 (over z, y, core).
Axes of the slice: x: 2, y: 2, z: 4, core: 2. Of those that a mesh axis runs over, the one named last changes fastest.
Arguments:
- embeddings: bfloat16 [16384, 512], P(('parts', 'row')), parts along dimension 0, may hold values from -6 to 6
- sizes: int32 [64], P('parts'), parts along dimension 0, may hold values from 1 to 2048, 8192 in all
- order: int32 [16384], P('parts'), parts along dimension 0, may hold values from 0 to 8191, each once
Outputs:
- similarity: float32 [16384], P(('parts', 'row')), parts along dimension 0
The draws below stay inside these ranges and needn't reach their ends.
There are 2 independent parts, one for each index of `parts`. The reference program is written for one: setup_inputs(seed, part) draws one part's arguments, and reference() takes and returns one part's arrays. A program takes and returns all parts, laid end to end along the dimension named above; each array names one. Nothing has to cross between parts.
Inputs may be any that keep to these rules, and one draw needn't show every extreme that they name: `sizes`: each cluster has 1 to 2048 items; they sum to 8192. `order`: each of 0 to 8191 once.
All inputs are finite; a program needn't handle non-finite values.
Results may differ from the reference program's by a relative error of at most 0.0014.
Values may be sent and summed in bfloat16 or wider, within the bound.
A program may use at most 64 MiB of HBM per device.

```python
import math
import jax
import jax.numpy as jnp
import numpy as np
from jax import lax

D = 512
ITEM_DEV = 512
ITEMS = 8192
CLUSTERS = 32
MOST = 2048
N_ROW = 16


def levels(key, dims, shards, least, top_value):
    def one(position, blocks):
        draws = jax.random.uniform(jax.random.fold_in(jax.random.fold_in(key, 6), position), (blocks,), jnp.float32, least / len(shards), top_value / len(shards))
        return jnp.repeat(jnp.exp(draws), dims[position] // blocks).reshape((-1,) + (1,) * (len(dims) - position - 1))

    factor_of = one(*shards[0])
    for cut in shards[1:]:
        factor_of = factor_of * one(*cut)
    return factor_of


def length_profile(number_of, total, limit, slope):
    portions = [(1 << 20) // math.isqrt(grade ** slope) + 1 for grade in range(2, number_of + 1)]
    surplus, given = total - limit - (number_of - 1), [1] * (number_of - 1)
    while surplus > 0:
        candidates = [i for i in range(number_of - 1) if given[i] < limit]
        whole, left = sum([portions[i] for i in candidates]), surplus
        for i in candidates:
            addition = min(limit - given[i], max(1, left * portions[i] // whole), surplus)
            given[i] = given[i] + addition
            surplus = surplus - addition
    return np.array([limit] + given)


def uneven_parts(stream_key, count, total, reach, lean):
    if count == 2:
        one = jax.random.randint(stream_key, (), max(1, total - reach), min(reach, total - 1) + 1)
        return jnp.stack([one, total - one])
    tallies = jnp.asarray(length_profile(count, total, reach, lean), jnp.int32)
    pairs = (count - 1) // 2
    source_of, taker = tallies[1:1 + 2 * pairs:2], tallies[2:2 + 2 * pairs:2]
    room = jnp.minimum(source_of - 1, reach - taker)
    shifted = jax.random.randint(jax.random.fold_in(stream_key, 1), (pairs,), 0, 1 << 20) % (room + 1)
    tallies = tallies.at[1:1 + 2 * pairs:2].set(source_of - shifted).at[2:2 + 2 * pairs:2].set(taker + shifted)
    return tallies[jax.random.permutation(jax.random.fold_in(stream_key, 2), count)]


def centred(stream_key, dims, deviation, reach, pieces=(), held_as=jnp.bfloat16):
    level = levels(stream_key, dims, pieces, -0.22, 0.18) if pieces else 1.0
    entries = jax.random.normal(stream_key, dims, jnp.float32) * deviation * level
    return jnp.minimum(jnp.maximum(entries, -reach), reach).astype(held_as)


def setup_inputs(seed: int = 0, part: int = 0) -> dict:
    key_list = jax.random.split(jax.random.key(seed), 4)
    own_keys = jax.random.split(jax.random.fold_in(key_list[3], part), 4)
    return {
        "embeddings": centred(own_keys[0], (ITEMS, D), 1.0, 6.0, ((0, 16),)),
        "sizes": uneven_parts(own_keys[1], CLUSTERS, ITEMS, MOST, 2).astype(jnp.int32),
        "order": jax.random.permutation(own_keys[2], ITEMS).astype(jnp.int32),
    }


def reference(embeddings, sizes, order):
    values = embeddings.astype(jnp.float32)
    unit = (values * lax.rsqrt(lax.optimization_barrier(jnp.sum(values * values, axis=1, keepdims=True)) + 1e-06)).astype(jnp.bfloat16)
    ends = jnp.cumsum(sizes).astype(jnp.int32)
    index = jnp.arange(ITEMS, dtype=jnp.int32)
    cluster = lax.optimization_barrier(jnp.sum((index[:, None] >= ends[None, :]).astype(jnp.int32), axis=1)).astype(jnp.int32)

    def block(number):
        start = (number * ITEM_DEV).astype(jnp.int32)
        rows = lax.dynamic_slice_in_dim(unit, start, ITEM_DEV, 0)
        mine = lax.dynamic_slice_in_dim(cluster, start, ITEM_DEV, 0)
        ranks = lax.dynamic_slice_in_dim(order, start, ITEM_DEV, 0)
        scores = jnp.dot(rows, unit.T, preferred_element_type=jnp.float32)
        keep = (mine[:, None] == cluster[None, :]) & (order[None, :] < ranks[:, None])
        return lax.optimization_barrier(jnp.max(jnp.where(keep, scores, jnp.float32(-1.0)), axis=1))
    result = lax.map(block, jnp.arange(N_ROW, dtype=jnp.int32))
    return result.reshape(ITEMS)
```

```python
import functools

import jax
import jax.numpy as jnp
from jax import lax
from jax.experimental import pallas as pl
from jax.experimental.pallas import tpu as pltpu
from jax.sharding import PartitionSpec as P

OWN, PART, ZED, WHY, FAR = range(5)
LANES = 128
CHUNKS = 4
BIG = 1e9
MESH = pl.DeviceIdType.MESH


def kernel(devices, x_ref, sizes_ref, order_ref, out_ref, raw, unit, col, acc_low, acc_high, ret, back,
           load_sem, send_sem, recv_sem, ret_send, ret_recv):
    rows, width = x_ref.shape
    tiles = rows // LANES
    piece = rows // CHUNKS
    clusters = sizes_ref.shape[0]
    parts_at = lax.axis_index("parts")
    me = lax.axis_index("row")
    core = lax.rem(me, 2)
    is_b = lax.rem(me // 2, 2)
    is_a = 1 - is_b
    plane = me // 4
    planes = devices // 4
    partner = me + 1 - 2 * core
    has_down = plane > 0
    has_up = plane < planes - 1
    other_chip = me - core + 2 - 4 * is_b

    def dev(index):
        return (parts_at, index)

    def both(*conditions):
        result = conditions[0]
        for condition in conditions[1:]:
            result = jnp.logical_and(result, condition)
        return result

    on_a, on_b = is_a == 1, is_b == 1
    first, second = core == 0, core == 1

    barrier = pltpu.get_barrier_semaphore()

    def greet(index):
        pl.semaphore_signal(barrier, inc=1, device_id=dev(index), device_id_type=MESH)

    greet(partner)
    greet(other_chip)
    greet(other_chip + 1)
    pl.when(has_down)(lambda: greet(me - 4))
    pl.when(has_up)(lambda: greet(me + 4))
    load = pltpu.make_async_copy(x_ref, raw.at[OWN], load_sem)
    load.start()
    pl.semaphore_wait(barrier, 3 + has_down.astype(jnp.int32) + has_up.astype(jnp.int32))

    def chunk(c):
        return pl.ds(c * piece, piece)

    def own_copy(slot, c, target):
        return pltpu.make_async_remote_copy(
            src_ref=x_ref.at[chunk(c)], dst_ref=raw.at[slot, chunk(c)],
            send_sem=send_sem.at[slot, c], recv_sem=recv_sem.at[slot, c],
            device_id=dev(target), device_id_type=MESH)

    def far_copy(c):
        return pltpu.make_async_remote_copy(
            src_ref=raw.at[WHY, chunk(c)], dst_ref=raw.at[FAR, chunk(c)],
            send_sem=send_sem.at[FAR, c], recv_sem=recv_sem.at[FAR, c],
            device_id=dev(partner), device_id_type=MESH)

    def part_copy():
        return pltpu.make_async_remote_copy(
            src_ref=x_ref, dst_ref=raw.at[PART],
            send_sem=send_sem.at[PART, 0], recv_sem=recv_sem.at[PART, 0],
            device_id=dev(partner), device_id_type=MESH)

    def ret_copy(slot, target):
        return pltpu.make_async_remote_copy(
            src_ref=back.at[slot], dst_ref=ret.at[slot],
            send_sem=ret_send.at[slot], recv_sem=ret_recv.at[slot],
            device_id=dev(target), device_id_type=MESH)

    z_target = jnp.where(on_b, me + 4, me - 4)
    z_source = jnp.where(on_b, me - 4, me + 4)
    sends_z = jnp.where(on_b, has_up, has_down)
    takes_z = jnp.where(on_b, has_down, has_up)
    sends_part = core == is_a
    takes_part = core == is_b
    sent = []

    for c in range(CHUNKS):
        @pl.when(sends_z)
        def _():
            own_copy(ZED, c, z_target).start()

        @pl.when(on_a)
        def _():
            own_copy(WHY, c, me + 2).start()

    @pl.when(sends_part)
    def _():
        part_copy().start()

    base = me - core - 2 * is_b
    block_of = [me, partner, z_source, base + core, base + 1 - core]
    sub = lax.broadcasted_iota(jnp.int32, (8, LANES), 0)
    lane = lax.broadcasted_iota(jnp.int32, (8, LANES), 1)
    last = jnp.zeros((8, LANES), jnp.int32)
    for slot, block in enumerate(block_of):
        last = jnp.where(sub == slot, (block + 1) * rows - 1, last)
    mine = me * rows + sub * LANES + lane

    def scan(c, carry):
        end, begin_last, end_last, begin_mine, end_mine = carry
        end = end + sizes_ref[c]
        done = end <= last
        begin_last = jnp.where(done, end, begin_last)
        end_last = jnp.where(done, end_last, jnp.minimum(end_last, end))
        done = end <= mine
        begin_mine = jnp.where(done, end, begin_mine)
        end_mine = jnp.where(done, end_mine, jnp.minimum(end_mine, end))
        return end, begin_last, end_last, begin_mine, end_mine

    zero = jnp.zeros((8, LANES), jnp.int32)
    top = jnp.full((8, LANES), 1 << 30, jnp.int32)
    carry = (jnp.int32(0), zero, top, zero, top)
    carry = lax.fori_loop(0, clusters, scan, carry, unroll=8)
    _, begin_last, end_last, begin_mine, end_mine = carry
    low = [begin_last[s:s + 1] for s in range(5)]
    high = [end_last[s:s + 1] for s in range(5)]
    lane_row = lax.broadcasted_iota(jnp.int32, (1, LANES), 1)

    def index_row(slot, t):
        return block_of[slot] * rows + t * LANES + lane_row

    def clipped(slot):
        return jnp.clip(block_of[slot], 0, devices - 1)

    def rank_row(slot, t):
        return order_ref[pl.ds(clipped(slot) * tiles + t, 1), :].astype(jnp.float32)

    def spread(row):
        return jnp.transpose(jnp.broadcast_to(row, (LANES, LANES)))

    for slot in range(5):
        for t in range(tiles):
            row = jnp.where(index_row(slot, t) >= low[slot], rank_row(slot, t), BIG)
            col[slot, pl.ds(t * LANES, LANES), :] = spread(row)
    for t in range(tiles):
        col[5, pl.ds(t * LANES, LANES), :] = spread(rank_row(OWN, t))
    acc_low[...] = jnp.full(acc_low.shape, -1.0, jnp.float32)
    acc_high[...] = jnp.full(acc_high.shape, -1.0, jnp.float32)

    def normalize(slot, start, count):
        at = pl.ds(start, count)
        values = raw[slot, at, :].astype(jnp.float32)
        total = jnp.sum(values * values, axis=1, keepdims=True)
        unit[slot, at, :] = (values * lax.rsqrt(total + 1e-06)).astype(jnp.bfloat16)

    def dot(a, b):
        return lax.dot_general(a, b, (((1,), (1,)), ((), ())), preferred_element_type=jnp.float32)

    def fold(x):
        return jnp.max(x.reshape(x.shape[0] // 8, 8, x.shape[1]), axis=0)

    def pair(lower, start, count, higher, first_col, cols):
        others = unit[higher, pl.ds(first_col, cols), :]
        ranks, inside = [], []
        for t in range(first_col // LANES, (first_col + cols) // LANES):
            within = index_row(higher, t) < high[lower]
            inside.append(within)
            ranks.append(jnp.where(within, rank_row(higher, t), 2 * BIG))

        def step(i, carry):
            at = pl.ds(pl.multiple_of(start + i * LANES, LANES), LANES)
            scores = dot(unit[lower, at, :], others)
            ranks_low = col[lower, at, :]
            best = acc_low[lower, at, :]
            result = []
            for n in range(len(ranks)):
                s = scores[:, n * LANES:(n + 1) * LANES]
                before = ranks_low < ranks[n]
                best = jnp.maximum(best, jnp.where(before, -1.0, s))
                result.append(jnp.maximum(carry[n], fold(jnp.where(before, s, -1.0))))
            acc_low[lower, at, :] = best
            return tuple(result)

        found = tuple(jnp.full((8, LANES), -1.0, jnp.float32) for _ in ranks)
        found = lax.fori_loop(0, count // LANES, step, found)
        for n in range(len(ranks)):
            at = pl.ds(first_col + n * LANES, LANES)
            masked = jnp.where(inside[n], found[n], -1.0)
            acc_high[higher, :, at] = jnp.maximum(acc_high[higher, :, at], masked)

    def within_own():
        others = unit[OWN]
        ranks = [rank_row(OWN, t) for t in range(tiles)]
        begins = [begin_mine[t:t + 1] for t in range(tiles)]
        ends = [end_mine[t:t + 1] for t in range(tiles)]

        def step(i, carry):
            at = pl.ds(pl.multiple_of(i * LANES, LANES), LANES)
            scores = dot(unit[OWN, at, :], others)
            ranks_low = col[5, at, :]
            index = me * rows + i * LANES + lax.broadcasted_iota(jnp.int32, (LANES, LANES), 0)
            result = []
            for n in range(tiles):
                s = scores[:, n * LANES:(n + 1) * LANES]
                keep = (ranks_low < ranks[n]) & (index >= begins[n]) & (index < ends[n])
                result.append(jnp.maximum(carry[n], fold(jnp.where(keep, s, -1.0))))
            return tuple(result)

        found = tuple(jnp.full((8, LANES), -1.0, jnp.float32) for _ in ranks)
        found = lax.fori_loop(0, tiles, step, found)
        for n in range(tiles):
            at = pl.ds(n * LANES, LANES)
            acc_high[OWN, :, at] = jnp.maximum(acc_high[OWN, :, at], found[n])

    def result_of(slot, lows=True):
        pieces = []
        for t in range(tiles):
            at = pl.ds(t * LANES, LANES)
            best = jnp.max(acc_high[slot, :, at], axis=0, keepdims=True)
            if lows:
                found = jnp.max(jnp.transpose(acc_low[slot, at, :]), axis=0, keepdims=True)
                best = jnp.maximum(best, jnp.where(index_row(slot, t) >= low[slot], found, -1.0))
            pieces.append(best)
        return jnp.concatenate(pieces, axis=1)

    load.wait()
    normalize(OWN, 0, rows)
    within_own()

    @pl.when(takes_part)
    def _():
        part_copy().wait_recv()
        normalize(PART, 0, rows)

    @pl.when(both(on_b, second))
    def _():
        pair(PART, 0, rows, OWN, 0, rows)

    @pl.when(both(on_a, first))
    def _():
        pair(OWN, 0, rows, PART, 0, rows)

    @pl.when(on_b)
    def _():
        for c in range(CHUNKS):
            start = c * piece
            own_copy(WHY, c, partner).wait_recv()
            far_copy(c).start()
            normalize(WHY, start, piece)
            pair(WHY, start, piece, OWN, 0, rows)

            @pl.when(has_down)
            def _():
                own_copy(ZED, c, partner).wait_recv()
                normalize(ZED, start, piece)
                pair(ZED, start, piece, OWN, 0, rows)

                @pl.when(second)
                def _():
                    pair(ZED, start, piece, PART, 0, rows)

                pair(ZED, start, piece, WHY, 0, start + piece)
                if c:
                    pair(ZED, 0, start, WHY, start, piece)

            far_copy(c).wait_recv()
            normalize(FAR, start, piece)
            pair(FAR, start, piece, OWN, 0, rows)

            @pl.when(has_down)
            def _():
                pair(ZED, start, piece, FAR, 0, start + piece)
                if c:
                    pair(ZED, 0, start, FAR, start, piece)

        back[2] = result_of(WHY)
        back[3] = result_of(FAR)

        @pl.when(first)
        def _():
            ret_copy(2, me - 2).start()
            pltpu.make_async_remote_copy(
                src_ref=back.at[3], dst_ref=ret.at[2], send_sem=ret_send.at[3], recv_sem=ret_recv.at[2],
                device_id=dev(me - 1), device_id_type=MESH).start()

        @pl.when(second)
        def _():
            pltpu.make_async_remote_copy(
                src_ref=back.at[2], dst_ref=ret.at[3], send_sem=ret_send.at[2], recv_sem=ret_recv.at[3],
                device_id=dev(me - 2), device_id_type=MESH).start()
            ret_copy(3, me - 3).start()
            back[1] = result_of(PART)
            ret_copy(1, partner).start()

        @pl.when(has_down)
        def _():
            back[0] = result_of(ZED)
            ret_copy(0, me - 4).start()

    @pl.when(on_a)
    def _():
        @pl.when(has_up)
        def _():
            for c in range(CHUNKS):
                start = c * piece
                own_copy(ZED, c, partner).wait_recv()
                normalize(ZED, start, piece)
                pair(OWN, 0, rows, ZED, start, piece)

                @pl.when(first)
                def _():
                    pair(PART, 0, rows, ZED, start, piece)

            back[0] = result_of(ZED, False)
            ret_copy(0, me + 4).start()

        @pl.when(first)
        def _():
            back[1] = result_of(PART)
            ret_copy(1, partner).start()

    out_ref[...] = result_of(OWN)

    def take(slot):
        ret_copy(slot, partner).wait_recv()
        out_ref[...] = jnp.maximum(out_ref[...], ret[slot])

    pl.when(sends_part)(lambda: take(1))
    pl.when(sends_z)(lambda: take(0))

    @pl.when(on_a)
    def _():
        take(2)
        take(3)

    for c in range(CHUNKS):
        pl.when(sends_z)(lambda: own_copy(ZED, c, partner).wait_send())
        pl.when(on_a)(lambda: own_copy(WHY, c, partner).wait_send())
        pl.when(on_b)(lambda: far_copy(c).wait_send())
    pl.when(sends_part)(lambda: part_copy().wait_send())
    pl.when(takes_part)(lambda: ret_copy(1, partner).wait_send())
    pl.when(takes_z)(lambda: ret_copy(0, partner).wait_send())

    @pl.when(on_b)
    def _():
        ret_copy(2, partner).wait_send()
        ret_copy(3, partner).wait_send()


def local(embeddings, sizes, order, devices):
    rows, width = embeddings.shape
    order = order.reshape(-1, LANES)
    result = pl.pallas_call(
        functools.partial(kernel, devices),
        out_shape=jax.ShapeDtypeStruct((1, rows), jnp.float32),
        in_specs=[
            pl.BlockSpec(memory_space=pl.ANY),
            pl.BlockSpec(memory_space=pltpu.SMEM),
            pl.BlockSpec(memory_space=pltpu.VMEM),
        ],
        out_specs=pl.BlockSpec(memory_space=pltpu.VMEM),
        scratch_shapes=[
            pltpu.VMEM((5, rows, width), jnp.bfloat16),
            pltpu.VMEM((5, rows, width), jnp.bfloat16),
            pltpu.VMEM((6, rows, LANES), jnp.float32),
            pltpu.VMEM((5, rows, LANES), jnp.float32),
            pltpu.VMEM((5, 8, rows), jnp.float32),
            pltpu.VMEM((4, 1, rows), jnp.float32),
            pltpu.VMEM((4, 1, rows), jnp.float32),
            pltpu.SemaphoreType.DMA,
            pltpu.SemaphoreType.DMA((5, CHUNKS)),
            pltpu.SemaphoreType.DMA((5, CHUNKS)),
            pltpu.SemaphoreType.DMA((4,)),
            pltpu.SemaphoreType.DMA((4,)),
        ],
        compiler_params=pltpu.CompilerParams(collective_id=0, has_side_effects=True),
    )(embeddings, sizes, order)
    return result.reshape(rows)


def solution(mesh):
    return jax.shard_map(
        functools.partial(local, devices=mesh.shape["row"]),
        mesh=mesh,
        in_specs=(P(("parts", "row"), None), P("parts"), P("parts")),
        out_specs=P(("parts", "row")),
        check_vma=False,
    )
```

```python
import functools

import jax
import jax.numpy as jnp
from jax import lax
from jax.experimental import pallas as pl
from jax.experimental.pallas import tpu as pltpu
from jax.sharding import PartitionSpec as P

OWN, PART, ZED, WHY, FAR = range(5)
LANES = 128
CHUNKS = 4
BIG = 1e9
MESH = pl.DeviceIdType.MESH


def kernel(devices, x_ref, sizes_hbm, order_hbm, out_ref, sizes_ref, order_ref, raw, unit, col, acc_low, acc_high, ret, back,
           load_sem, small_sem, send_sem, recv_sem, ret_send, ret_recv):
    rows, width = x_ref.shape
    tiles = rows // LANES
    piece = rows // CHUNKS
    clusters = sizes_ref.shape[0]
    parts_at = lax.axis_index("parts")
    me = lax.axis_index("row")
    core = lax.rem(me, 2)
    is_b = lax.rem(me // 2, 2)
    is_a = 1 - is_b
    plane = me // 4
    planes = devices // 4
    partner = me + 1 - 2 * core
    has_down = plane > 0
    has_up = plane < planes - 1
    other_chip = me - core + 2 - 4 * is_b

    def dev(index):
        return (parts_at, index)

    def both(*conditions):
        result = conditions[0]
        for condition in conditions[1:]:
            result = jnp.logical_and(result, condition)
        return result

    on_a, on_b = is_a == 1, is_b == 1
    first, second = core == 0, core == 1

    barrier = pltpu.get_barrier_semaphore()

    def greet(index):
        pl.semaphore_signal(barrier, inc=1, device_id=dev(index), device_id_type=MESH)

    greet(partner)
    greet(other_chip)
    greet(other_chip + 1)
    pl.when(has_down)(lambda: greet(me - 4))
    pl.when(has_up)(lambda: greet(me + 4))
    load = pltpu.make_async_copy(x_ref, raw.at[OWN], load_sem)
    load.start()
    load_sizes = pltpu.make_async_copy(sizes_hbm, sizes_ref, small_sem.at[0])
    load_sizes.start()
    load_order = pltpu.make_async_copy(order_hbm, order_ref, small_sem.at[1])
    load_order.start()
    pl.semaphore_wait(barrier, 3 + has_down.astype(jnp.int32) + has_up.astype(jnp.int32))

    def chunk(c):
        return pl.ds(c * piece, piece)

    def own_copy(slot, c, target):
        return pltpu.make_async_remote_copy(
            src_ref=x_ref.at[chunk(c)], dst_ref=raw.at[slot, chunk(c)],
            send_sem=send_sem.at[slot, c], recv_sem=recv_sem.at[slot, c],
            device_id=dev(target), device_id_type=MESH)

    def far_copy(c):
        return pltpu.make_async_remote_copy(
            src_ref=raw.at[WHY, chunk(c)], dst_ref=raw.at[FAR, chunk(c)],
            send_sem=send_sem.at[FAR, c], recv_sem=recv_sem.at[FAR, c],
            device_id=dev(partner), device_id_type=MESH)

    def part_copy():
        return pltpu.make_async_remote_copy(
            src_ref=x_ref, dst_ref=raw.at[PART],
            send_sem=send_sem.at[PART, 0], recv_sem=recv_sem.at[PART, 0],
            device_id=dev(partner), device_id_type=MESH)

    def ret_copy(slot, target):
        return pltpu.make_async_remote_copy(
            src_ref=back.at[slot], dst_ref=ret.at[slot],
            send_sem=ret_send.at[slot], recv_sem=ret_recv.at[slot],
            device_id=dev(target), device_id_type=MESH)

    z_target = jnp.where(on_b, me + 4, me - 4)
    z_source = jnp.where(on_b, me - 4, me + 4)
    sends_z = jnp.where(on_b, has_up, has_down)
    takes_z = jnp.where(on_b, has_down, has_up)
    sends_part = core == is_a
    takes_part = core == is_b
    sent = []

    for c in range(CHUNKS):
        @pl.when(sends_z)
        def _():
            own_copy(ZED, c, z_target).start()

        @pl.when(on_a)
        def _():
            own_copy(WHY, c, me + 2).start()

    @pl.when(sends_part)
    def _():
        part_copy().start()

    load_sizes.wait()
    load_order.wait()

    base = me - core - 2 * is_b
    block_of = [me, partner, z_source, base + core, base + 1 - core]
    sub = lax.broadcasted_iota(jnp.int32, (8, LANES), 0)
    lane = lax.broadcasted_iota(jnp.int32, (8, LANES), 1)
    last = jnp.zeros((8, LANES), jnp.int32)
    for slot, block in enumerate(block_of):
        last = jnp.where(sub == slot, (block + 1) * rows - 1, last)
    mine = me * rows + sub * LANES + lane

    def scan(c, carry):
        end, begin_last, end_last, begin_mine, end_mine = carry
        end = end + sizes_ref[c]
        done = end <= last
        begin_last = jnp.where(done, end, begin_last)
        end_last = jnp.where(done, end_last, jnp.minimum(end_last, end))
        done = end <= mine
        begin_mine = jnp.where(done, end, begin_mine)
        end_mine = jnp.where(done, end_mine, jnp.minimum(end_mine, end))
        return end, begin_last, end_last, begin_mine, end_mine

    zero = jnp.zeros((8, LANES), jnp.int32)
    top = jnp.full((8, LANES), 1 << 30, jnp.int32)
    carry = (jnp.int32(0), zero, top, zero, top)
    carry = lax.fori_loop(0, clusters, scan, carry, unroll=8)
    _, begin_last, end_last, begin_mine, end_mine = carry
    low = [begin_last[s:s + 1] for s in range(5)]
    high = [end_last[s:s + 1] for s in range(5)]
    lane_row = lax.broadcasted_iota(jnp.int32, (1, LANES), 1)

    def index_row(slot, t):
        return block_of[slot] * rows + t * LANES + lane_row

    def clipped(slot):
        return jnp.clip(block_of[slot], 0, devices - 1)

    def rank_row(slot, t):
        return order_ref[pl.ds(clipped(slot) * tiles + t, 1), :].astype(jnp.float32)

    def spread(row):
        return jnp.transpose(jnp.broadcast_to(row, (LANES, LANES)))

    for slot in range(5):
        for t in range(tiles):
            row = jnp.where(index_row(slot, t) >= low[slot], rank_row(slot, t), BIG)
            col[slot, pl.ds(t * LANES, LANES), :] = spread(row)
    for t in range(tiles):
        col[5, pl.ds(t * LANES, LANES), :] = spread(rank_row(OWN, t))
    acc_low[...] = jnp.full(acc_low.shape, -1.0, jnp.float32)
    acc_high[...] = jnp.full(acc_high.shape, -1.0, jnp.float32)

    def normalize(slot, start, count):
        at = pl.ds(start, count)
        values = raw[slot, at, :].astype(jnp.float32)
        total = jnp.sum(values * values, axis=1, keepdims=True)
        unit[slot, at, :] = (values * lax.rsqrt(total + 1e-06)).astype(jnp.bfloat16)

    def dot(a, b):
        return lax.dot_general(a, b, (((1,), (1,)), ((), ())), preferred_element_type=jnp.float32)

    def fold(x):
        return jnp.max(x.reshape(x.shape[0] // 8, 8, x.shape[1]), axis=0)

    def pair(lower, start, count, higher, first_col, cols):
        others = unit[higher, pl.ds(first_col, cols), :]
        ranks, inside = [], []
        for t in range(first_col // LANES, (first_col + cols) // LANES):
            within = index_row(higher, t) < high[lower]
            inside.append(within)
            ranks.append(jnp.where(within, rank_row(higher, t), 2 * BIG))

        def step(i, carry):
            at = pl.ds(pl.multiple_of(start + i * LANES, LANES), LANES)
            scores = dot(unit[lower, at, :], others)
            ranks_low = col[lower, at, :]
            best = acc_low[lower, at, :]
            result = []
            for n in range(len(ranks)):
                s = scores[:, n * LANES:(n + 1) * LANES]
                before = ranks_low < ranks[n]
                best = jnp.maximum(best, jnp.where(before, -1.0, s))
                result.append(jnp.maximum(carry[n], fold(jnp.where(before, s, -1.0))))
            acc_low[lower, at, :] = best
            return tuple(result)

        found = tuple(jnp.full((8, LANES), -1.0, jnp.float32) for _ in ranks)
        found = lax.fori_loop(0, count // LANES, step, found)
        for n in range(len(ranks)):
            at = pl.ds(first_col + n * LANES, LANES)
            masked = jnp.where(inside[n], found[n], -1.0)
            acc_high[higher, :, at] = jnp.maximum(acc_high[higher, :, at], masked)

    def within_own():
        others = unit[OWN]
        ranks = [rank_row(OWN, t) for t in range(tiles)]
        begins = [begin_mine[t:t + 1] for t in range(tiles)]
        ends = [end_mine[t:t + 1] for t in range(tiles)]

        def step(i, carry):
            at = pl.ds(pl.multiple_of(i * LANES, LANES), LANES)
            scores = dot(unit[OWN, at, :], others)
            ranks_low = col[5, at, :]
            index = me * rows + i * LANES + lax.broadcasted_iota(jnp.int32, (LANES, LANES), 0)
            result = []
            for n in range(tiles):
                s = scores[:, n * LANES:(n + 1) * LANES]
                keep = (ranks_low < ranks[n]) & (index >= begins[n]) & (index < ends[n])
                result.append(jnp.maximum(carry[n], fold(jnp.where(keep, s, -1.0))))
            return tuple(result)

        found = tuple(jnp.full((8, LANES), -1.0, jnp.float32) for _ in ranks)
        found = lax.fori_loop(0, tiles, step, found)
        for n in range(tiles):
            at = pl.ds(n * LANES, LANES)
            acc_high[OWN, :, at] = jnp.maximum(acc_high[OWN, :, at], found[n])

    def result_of(slot, lows=True):
        pieces = []
        for t in range(tiles):
            at = pl.ds(t * LANES, LANES)
            best = jnp.max(acc_high[slot, :, at], axis=0, keepdims=True)
            if lows:
                found = jnp.max(jnp.transpose(acc_low[slot, at, :]), axis=0, keepdims=True)
                best = jnp.maximum(best, jnp.where(index_row(slot, t) >= low[slot], found, -1.0))
            pieces.append(best)
        return jnp.concatenate(pieces, axis=1)

    load.wait()
    normalize(OWN, 0, rows)
    within_own()

    @pl.when(takes_part)
    def _():
        part_copy().wait_recv()
        normalize(PART, 0, rows)

    @pl.when(both(on_b, second))
    def _():
        pair(PART, 0, rows, OWN, 0, rows)

    @pl.when(both(on_a, first))
    def _():
        pair(OWN, 0, rows, PART, 0, rows)

    @pl.when(on_b)
    def _():
        for c in range(CHUNKS):
            start = c * piece
            own_copy(WHY, c, partner).wait_recv()
            far_copy(c).start()
            normalize(WHY, start, piece)
            pair(WHY, start, piece, OWN, 0, rows)

            @pl.when(has_down)
            def _():
                own_copy(ZED, c, partner).wait_recv()
                normalize(ZED, start, piece)
                pair(ZED, start, piece, OWN, 0, rows)

                @pl.when(second)
                def _():
                    pair(ZED, start, piece, PART, 0, rows)

                pair(ZED, start, piece, WHY, 0, start + piece)
                if c:
                    pair(ZED, 0, start, WHY, start, piece)

            if c == CHUNKS - 1:
                back[2] = result_of(WHY)

                @pl.when(first)
                def _():
                    ret_copy(2, me - 2).start()

                @pl.when(second)
                def _():
                    pltpu.make_async_remote_copy(
                        src_ref=back.at[2], dst_ref=ret.at[3], send_sem=ret_send.at[2],
                        recv_sem=ret_recv.at[3], device_id=dev(me - 2), device_id_type=MESH).start()
                    back[1] = result_of(PART)
                    ret_copy(1, partner).start()

            far_copy(c).wait_recv()
            normalize(FAR, start, piece)
            pair(FAR, start, piece, OWN, 0, rows)

            @pl.when(has_down)
            def _():
                pair(ZED, start, piece, FAR, 0, start + piece)
                if c:
                    pair(ZED, 0, start, FAR, start, piece)

        back[3] = result_of(FAR)

        @pl.when(first)
        def _():
            pltpu.make_async_remote_copy(
                src_ref=back.at[3], dst_ref=ret.at[2], send_sem=ret_send.at[3], recv_sem=ret_recv.at[2],
                device_id=dev(me - 1), device_id_type=MESH).start()

        @pl.when(second)
        def _():
            ret_copy(3, me - 3).start()

        @pl.when(has_down)
        def _():
            back[0] = result_of(ZED)
            ret_copy(0, me - 4).start()

    @pl.when(on_a)
    def _():
        @pl.when(has_up)
        def _():
            for c in range(CHUNKS):
                start = c * piece
                own_copy(ZED, c, partner).wait_recv()
                normalize(ZED, start, piece)
                pair(OWN, 0, rows, ZED, start, piece)

                @pl.when(first)
                def _():
                    pair(PART, 0, rows, ZED, start, piece)

            back[0] = result_of(ZED, False)
            ret_copy(0, me + 4).start()

        @pl.when(first)
        def _():
            back[1] = result_of(PART)
            ret_copy(1, partner).start()

    out_ref[...] = result_of(OWN)

    def take(slot):
        ret_copy(slot, partner).wait_recv()
        out_ref[...] = jnp.maximum(out_ref[...], ret[slot])

    pl.when(sends_part)(lambda: take(1))
    pl.when(sends_z)(lambda: take(0))

    @pl.when(on_a)
    def _():
        take(2)
        take(3)

    for c in range(CHUNKS):
        pl.when(sends_z)(lambda: own_copy(ZED, c, partner).wait_send())
        pl.when(on_a)(lambda: own_copy(WHY, c, partner).wait_send())
        pl.when(on_b)(lambda: far_copy(c).wait_send())
    pl.when(sends_part)(lambda: part_copy().wait_send())
    pl.when(takes_part)(lambda: ret_copy(1, partner).wait_send())
    pl.when(takes_z)(lambda: ret_copy(0, partner).wait_send())

    @pl.when(on_b)
    def _():
        ret_copy(2, partner).wait_send()
        ret_copy(3, partner).wait_send()


def local(embeddings, sizes, order, devices):
    rows, width = embeddings.shape
    order = order.reshape(-1, LANES)
    result = pl.pallas_call(
        functools.partial(kernel, devices),
        out_shape=pltpu.VMEM((1, rows), jnp.float32),
        in_specs=[
            pl.BlockSpec(memory_space=pl.ANY),
            pl.BlockSpec(memory_space=pl.ANY),
            pl.BlockSpec(memory_space=pl.ANY),
        ],
        out_specs=pl.BlockSpec(memory_space=pltpu.VMEM),
        scratch_shapes=[
            pltpu.SMEM(sizes.shape, jnp.int32),
            pltpu.VMEM(order.shape, jnp.int32),
            pltpu.VMEM((5, rows, width), jnp.bfloat16),
            pltpu.VMEM((5, rows, width), jnp.bfloat16),
            pltpu.VMEM((6, rows, LANES), jnp.float32),
            pltpu.VMEM((5, rows, LANES), jnp.float32),
            pltpu.VMEM((5, 8, rows), jnp.float32),
            pltpu.VMEM((4, 1, rows), jnp.float32),
            pltpu.VMEM((4, 1, rows), jnp.float32),
            pltpu.SemaphoreType.DMA,
            pltpu.SemaphoreType.DMA((2,)),
            pltpu.SemaphoreType.DMA((5, CHUNKS)),
            pltpu.SemaphoreType.DMA((5, CHUNKS)),
            pltpu.SemaphoreType.DMA((4,)),
            pltpu.SemaphoreType.DMA((4,)),
        ],
        compiler_params=pltpu.CompilerParams(collective_id=0, has_side_effects=True),
    )(embeddings, sizes, order)
    return result.reshape(rows)


def solution(mesh):
    return jax.shard_map(
        functools.partial(local, devices=mesh.shape["row"]),
        mesh=mesh,
        in_specs=(P(("parts", "row"), None), P("parts"), P("parts")),
        out_specs=P(("parts", "row")),
        check_vma=False,
    )
```

```python
import functools

import jax
import jax.numpy as jnp
from jax import lax
from jax.experimental import pallas as pl
from jax.experimental.pallas import tpu as pltpu
from jax.sharding import PartitionSpec as P

OWN, PART, ZED, WHY, FAR = range(5)
LANES = 128
CHUNKS = 4
BIG = 1e9
MESH = pl.DeviceIdType.MESH


def kernel(devices, x_ref, sizes_hbm, order_hbm, out_ref, sizes_ref, order_ref, raw, unit, col, acc_low, acc_high, ret, back,
           load_sem, small_sem, send_sem, recv_sem, ret_send, ret_recv):
    rows, width = x_ref.shape
    tiles = rows // LANES
    piece = rows // CHUNKS
    clusters = sizes_ref.shape[0]
    parts_at = lax.axis_index("parts")
    me = lax.axis_index("row")
    core = lax.rem(me, 2)
    is_b = lax.rem(me // 2, 2)
    is_a = 1 - is_b
    plane = me // 4
    planes = devices // 4
    partner = me + 1 - 2 * core
    has_down = plane > 0
    has_up = plane < planes - 1
    other_chip = me - core + 2 - 4 * is_b

    def dev(index):
        return (parts_at, index)

    def both(*conditions):
        result = conditions[0]
        for condition in conditions[1:]:
            result = jnp.logical_and(result, condition)
        return result

    on_a, on_b = is_a == 1, is_b == 1
    first, second = core == 0, core == 1

    barrier = pltpu.get_barrier_semaphore()

    def greet(index):
        pl.semaphore_signal(barrier, inc=1, device_id=dev(index), device_id_type=MESH)

    greet(partner)
    greet(other_chip)
    greet(other_chip + 1)
    pl.when(has_down)(lambda: greet(me - 4))
    pl.when(has_up)(lambda: greet(me + 4))
    load = pltpu.make_async_copy(x_ref, raw.at[OWN], load_sem)
    load.start()
    load_sizes = pltpu.make_async_copy(sizes_hbm, sizes_ref, small_sem.at[0])
    load_sizes.start()
    load_order = pltpu.make_async_copy(order_hbm, order_ref, small_sem.at[1])
    load_order.start()
    pl.semaphore_wait(barrier, 3 + has_down.astype(jnp.int32) + has_up.astype(jnp.int32))

    load.wait()

    def chunk(c):
        return pl.ds(c * piece, piece)

    def own_copy(slot, c, target):
        return pltpu.make_async_remote_copy(
            src_ref=raw.at[OWN, chunk(c)], dst_ref=raw.at[slot, chunk(c)],
            send_sem=send_sem.at[slot, c], recv_sem=recv_sem.at[slot, c],
            device_id=dev(target), device_id_type=MESH)

    def far_copy(c):
        return pltpu.make_async_remote_copy(
            src_ref=raw.at[WHY, chunk(c)], dst_ref=raw.at[FAR, chunk(c)],
            send_sem=send_sem.at[FAR, c], recv_sem=recv_sem.at[FAR, c],
            device_id=dev(partner), device_id_type=MESH)

    def part_copy():
        return pltpu.make_async_remote_copy(
            src_ref=raw.at[OWN], dst_ref=raw.at[PART],
            send_sem=send_sem.at[PART, 0], recv_sem=recv_sem.at[PART, 0],
            device_id=dev(partner), device_id_type=MESH)

    def ret_copy(slot, target):
        return pltpu.make_async_remote_copy(
            src_ref=back.at[slot], dst_ref=ret.at[slot],
            send_sem=ret_send.at[slot], recv_sem=ret_recv.at[slot],
            device_id=dev(target), device_id_type=MESH)

    z_target = jnp.where(on_b, me + 4, me - 4)
    z_source = jnp.where(on_b, me - 4, me + 4)
    sends_z = jnp.where(on_b, has_up, has_down)
    takes_z = jnp.where(on_b, has_down, has_up)
    sends_part = core == is_a
    takes_part = core == is_b
    sent = []

    @pl.when(on_a)
    def _():
        for c in range(CHUNKS):
            own_copy(WHY, c, me + 2).start()

    @pl.when(sends_z)
    def _():
        for c in range(CHUNKS):
            own_copy(ZED, c, z_target).start()

    @pl.when(sends_part)
    def _():
        part_copy().start()

    load_sizes.wait()
    load_order.wait()

    base = me - core - 2 * is_b
    block_of = [me, partner, z_source, base + core, base + 1 - core]
    sub = lax.broadcasted_iota(jnp.int32, (8, LANES), 0)
    lane = lax.broadcasted_iota(jnp.int32, (8, LANES), 1)
    last = jnp.zeros((8, LANES), jnp.int32)
    for slot, block in enumerate(block_of):
        last = jnp.where(sub == slot, (block + 1) * rows - 1, last)
    mine = me * rows + sub * LANES + lane

    def scan(c, carry):
        end, begin_last, end_last, begin_mine, end_mine = carry
        end = end + sizes_ref[c]
        done = end <= last
        begin_last = jnp.where(done, end, begin_last)
        end_last = jnp.where(done, end_last, jnp.minimum(end_last, end))
        done = end <= mine
        begin_mine = jnp.where(done, end, begin_mine)
        end_mine = jnp.where(done, end_mine, jnp.minimum(end_mine, end))
        return end, begin_last, end_last, begin_mine, end_mine

    zero = jnp.zeros((8, LANES), jnp.int32)
    top = jnp.full((8, LANES), 1 << 30, jnp.int32)
    carry = (jnp.int32(0), zero, top, zero, top)
    carry = lax.fori_loop(0, clusters, scan, carry, unroll=8)
    _, begin_last, end_last, begin_mine, end_mine = carry
    low = [begin_last[s:s + 1] for s in range(5)]
    high = [end_last[s:s + 1] for s in range(5)]
    lane_row = lax.broadcasted_iota(jnp.int32, (1, LANES), 1)

    def index_row(slot, t):
        return block_of[slot] * rows + t * LANES + lane_row

    def clipped(slot):
        return jnp.clip(block_of[slot], 0, devices - 1)

    def rank_row(slot, t):
        return order_ref[pl.ds(clipped(slot) * tiles + t, 1), :].astype(jnp.float32)

    def spread(row):
        return jnp.transpose(jnp.broadcast_to(row, (LANES, LANES)))

    for slot in range(5):
        for t in range(tiles):
            row = jnp.where(index_row(slot, t) >= low[slot], rank_row(slot, t), BIG)
            col[slot, pl.ds(t * LANES, LANES), :] = spread(row)
    for t in range(tiles):
        col[5, pl.ds(t * LANES, LANES), :] = spread(rank_row(OWN, t))
    acc_low[...] = jnp.full(acc_low.shape, -1.0, jnp.float32)
    acc_high[...] = jnp.full(acc_high.shape, -1.0, jnp.float32)

    def normalize(slot, start, count):
        at = pl.ds(start, count)
        values = raw[slot, at, :].astype(jnp.float32)
        total = jnp.sum(values * values, axis=1, keepdims=True)
        unit[slot, at, :] = (values * lax.rsqrt(total + 1e-06)).astype(jnp.bfloat16)

    def dot(a, b):
        return lax.dot_general(a, b, (((1,), (1,)), ((), ())), preferred_element_type=jnp.float32)

    def fold(x):
        return jnp.max(x.reshape(x.shape[0] // 8, 8, x.shape[1]), axis=0)

    def pair(lower, start, count, higher, first_col, cols):
        others = unit[higher, pl.ds(first_col, cols), :]
        ranks, inside = [], []
        for t in range(first_col // LANES, (first_col + cols) // LANES):
            within = index_row(higher, t) < high[lower]
            inside.append(within)
            ranks.append(jnp.where(within, rank_row(higher, t), 2 * BIG))

        def step(i, carry):
            at = pl.ds(pl.multiple_of(start + i * LANES, LANES), LANES)
            scores = dot(unit[lower, at, :], others)
            ranks_low = col[lower, at, :]
            best = acc_low[lower, at, :]
            result = []
            for n in range(len(ranks)):
                s = scores[:, n * LANES:(n + 1) * LANES]
                before = ranks_low < ranks[n]
                best = jnp.maximum(best, jnp.where(before, -1.0, s))
                result.append(jnp.maximum(carry[n], fold(jnp.where(before, s, -1.0))))
            acc_low[lower, at, :] = best
            return tuple(result)

        found = tuple(jnp.full((8, LANES), -1.0, jnp.float32) for _ in ranks)
        found = lax.fori_loop(0, count // LANES, step, found)
        for n in range(len(ranks)):
            at = pl.ds(first_col + n * LANES, LANES)
            masked = jnp.where(inside[n], found[n], -1.0)
            acc_high[higher, :, at] = jnp.maximum(acc_high[higher, :, at], masked)

    def within_own():
        others = unit[OWN]
        ranks = [rank_row(OWN, t) for t in range(tiles)]
        begins = [begin_mine[t:t + 1] for t in range(tiles)]
        ends = [end_mine[t:t + 1] for t in range(tiles)]

        def step(i, carry):
            at = pl.ds(pl.multiple_of(i * LANES, LANES), LANES)
            scores = dot(unit[OWN, at, :], others)
            ranks_low = col[5, at, :]
            index = me * rows + i * LANES + lax.broadcasted_iota(jnp.int32, (LANES, LANES), 0)
            result = []
            for n in range(tiles):
                s = scores[:, n * LANES:(n + 1) * LANES]
                keep = (ranks_low < ranks[n]) & (index >= begins[n]) & (index < ends[n])
                result.append(jnp.maximum(carry[n], fold(jnp.where(keep, s, -1.0))))
            return tuple(result)

        found = tuple(jnp.full((8, LANES), -1.0, jnp.float32) for _ in ranks)
        found = lax.fori_loop(0, tiles, step, found)
        for n in range(tiles):
            at = pl.ds(n * LANES, LANES)
            acc_high[OWN, :, at] = jnp.maximum(acc_high[OWN, :, at], found[n])

    def result_of(slot, lows=True):
        pieces = []
        for t in range(tiles):
            at = pl.ds(t * LANES, LANES)
            best = jnp.max(acc_high[slot, :, at], axis=0, keepdims=True)
            if lows:
                found = jnp.max(jnp.transpose(acc_low[slot, at, :]), axis=0, keepdims=True)
                best = jnp.maximum(best, jnp.where(index_row(slot, t) >= low[slot], found, -1.0))
            pieces.append(best)
        return jnp.concatenate(pieces, axis=1)

    normalize(OWN, 0, rows)
    within_own()

    @pl.when(takes_part)
    def _():
        part_copy().wait_recv()
        normalize(PART, 0, rows)

    @pl.when(both(on_b, second))
    def _():
        pair(PART, 0, rows, OWN, 0, rows)

    @pl.when(both(on_a, first))
    def _():
        pair(OWN, 0, rows, PART, 0, rows)

    @pl.when(on_b)
    def _():
        for c in range(CHUNKS):
            start = c * piece
            own_copy(WHY, c, partner).wait_recv()
            far_copy(c).start()
            normalize(WHY, start, piece)
            pair(WHY, start, piece, OWN, 0, rows)

            @pl.when(has_down)
            def _():
                own_copy(ZED, c, partner).wait_recv()
                normalize(ZED, start, piece)
                pair(ZED, start, piece, OWN, 0, rows)

                @pl.when(second)
                def _():
                    pair(ZED, start, piece, PART, 0, rows)

                pair(ZED, start, piece, WHY, 0, start + piece)
                if c:
                    pair(ZED, 0, start, WHY, start, piece)

            if c == CHUNKS - 1:
                back[2] = result_of(WHY)

                @pl.when(first)
                def _():
                    ret_copy(2, me - 2).start()

                @pl.when(second)
                def _():
                    pltpu.make_async_remote_copy(
                        src_ref=back.at[2], dst_ref=ret.at[3], send_sem=ret_send.at[2],
                        recv_sem=ret_recv.at[3], device_id=dev(me - 2), device_id_type=MESH).start()
                    back[1] = result_of(PART)
                    ret_copy(1, partner).start()

            far_copy(c).wait_recv()
            normalize(FAR, start, piece)
            pair(FAR, start, piece, OWN, 0, rows)

            @pl.when(has_down)
            def _():
                pair(ZED, start, piece, FAR, 0, start + piece)
                if c:
                    pair(ZED, 0, start, FAR, start, piece)

        back[3] = result_of(FAR)

        @pl.when(first)
        def _():
            pltpu.make_async_remote_copy(
                src_ref=back.at[3], dst_ref=ret.at[2], send_sem=ret_send.at[3], recv_sem=ret_recv.at[2],
                device_id=dev(me - 1), device_id_type=MESH).start()

        @pl.when(second)
        def _():
            ret_copy(3, me - 3).start()

        @pl.when(has_down)
        def _():
            back[0] = result_of(ZED)
            ret_copy(0, me - 4).start()

    @pl.when(on_a)
    def _():
        @pl.when(has_up)
        def _():
            for c in range(CHUNKS):
                start = c * piece
                own_copy(ZED, c, partner).wait_recv()
                normalize(ZED, start, piece)
                pair(OWN, 0, rows, ZED, start, piece)

                @pl.when(first)
                def _():
                    pair(PART, 0, rows, ZED, start, piece)

            back[0] = result_of(ZED, False)
            ret_copy(0, me + 4).start()

        @pl.when(first)
        def _():
            back[1] = result_of(PART)
            ret_copy(1, partner).start()

    out_ref[...] = result_of(OWN)

    def take(slot):
        ret_copy(slot, partner).wait_recv()
        out_ref[...] = jnp.maximum(out_ref[...], ret[slot])

    pl.when(sends_part)(lambda: take(1))
    pl.when(sends_z)(lambda: take(0))

    @pl.when(on_a)
    def _():
        take(2)
        take(3)

    for c in range(CHUNKS):
        pl.when(sends_z)(lambda: own_copy(ZED, c, partner).wait_send())
        pl.when(on_a)(lambda: own_copy(WHY, c, partner).wait_send())
        pl.when(on_b)(lambda: far_copy(c).wait_send())
    pl.when(sends_part)(lambda: part_copy().wait_send())
    pl.when(takes_part)(lambda: ret_copy(1, partner).wait_send())
    pl.when(takes_z)(lambda: ret_copy(0, partner).wait_send())

    @pl.when(on_b)
    def _():
        ret_copy(2, partner).wait_send()
        ret_copy(3, partner).wait_send()


def local(embeddings, sizes, order, devices):
    rows, width = embeddings.shape
    order = order.reshape(-1, LANES)
    result = pl.pallas_call(
        functools.partial(kernel, devices),
        out_shape=pltpu.VMEM((1, rows), jnp.float32),
        in_specs=[
            pl.BlockSpec(memory_space=pl.ANY),
            pl.BlockSpec(memory_space=pl.ANY),
            pl.BlockSpec(memory_space=pl.ANY),
        ],
        out_specs=pl.BlockSpec(memory_space=pltpu.VMEM),
        scratch_shapes=[
            pltpu.SMEM(sizes.shape, jnp.int32),
            pltpu.VMEM(order.shape, jnp.int32),
            pltpu.VMEM((5, rows, width), jnp.bfloat16),
            pltpu.VMEM((5, rows, width), jnp.bfloat16),
            pltpu.VMEM((6, rows, LANES), jnp.float32),
            pltpu.VMEM((5, rows, LANES), jnp.float32),
            pltpu.VMEM((5, 8, rows), jnp.float32),
            pltpu.VMEM((4, 1, rows), jnp.float32),
            pltpu.VMEM((4, 1, rows), jnp.float32),
            pltpu.SemaphoreType.DMA,
            pltpu.SemaphoreType.DMA((2,)),
            pltpu.SemaphoreType.DMA((5, CHUNKS)),
            pltpu.SemaphoreType.DMA((5, CHUNKS)),
            pltpu.SemaphoreType.DMA((4,)),
            pltpu.SemaphoreType.DMA((4,)),
        ],
        compiler_params=pltpu.CompilerParams(collective_id=0, has_side_effects=True),
    )(embeddings, sizes, order)
    return result.reshape(rows)


def solution(mesh):
    return jax.shard_map(
        functools.partial(local, devices=mesh.shape["row"]),
        mesh=mesh,
        in_specs=(P(("parts", "row"), None), P("parts"), P("parts")),
        out_specs=P(("parts", "row")),
        check_vma=False,
    )
```

```python
import functools

import jax
import jax.numpy as jnp
from jax import lax
from jax.experimental import pallas as pl
from jax.experimental.pallas import tpu as pltpu
from jax.sharding import PartitionSpec as P

OWN, PART, ZED, WHY, FAR = range(5)
LANES = 128
CHUNKS = 4
BIG = 1e9
MESH = pl.DeviceIdType.MESH


def kernel(devices, x_ref, sizes_hbm, order_hbm, out_ref, sizes_ref, order_ref, raw, unit, col, acc_low, acc_high, ret, back,
           load_sem, small_sem, send_sem, recv_sem, ret_send, ret_recv):
    rows, width = x_ref.shape
    tiles = rows // LANES
    piece = rows // CHUNKS
    clusters = sizes_ref.shape[0]
    parts_at = lax.axis_index("parts")
    me = lax.axis_index("row")
    core = lax.rem(me, 2)
    is_b = lax.rem(me // 2, 2)
    is_a = 1 - is_b
    plane = me // 4
    planes = devices // 4
    partner = me + 1 - 2 * core
    has_down = plane > 0
    has_up = plane < planes - 1
    other_chip = me - core + 2 - 4 * is_b

    def dev(index):
        return (parts_at, index)

    def both(*conditions):
        result = conditions[0]
        for condition in conditions[1:]:
            result = jnp.logical_and(result, condition)
        return result

    on_a, on_b = is_a == 1, is_b == 1
    first, second = core == 0, core == 1

    barrier = pltpu.get_barrier_semaphore()

    def greet(index):
        pl.semaphore_signal(barrier, inc=1, device_id=dev(index), device_id_type=MESH)

    greet(partner)
    greet(other_chip)
    greet(other_chip + 1)
    pl.when(has_down)(lambda: greet(me - 4))
    pl.when(has_up)(lambda: greet(me + 4))
    load = pltpu.make_async_copy(x_ref, raw.at[OWN], load_sem)
    load.start()
    load_sizes = pltpu.make_async_copy(sizes_hbm, sizes_ref, small_sem.at[0])
    load_sizes.start()
    load_order = pltpu.make_async_copy(order_hbm, order_ref, small_sem.at[1])
    load_order.start()
    z_source = jnp.where(on_b, me - 4, me + 4)
    load_sizes.wait()
    load_order.wait()

    base = me - core - 2 * is_b
    block_of = [me, partner, z_source, base + core, base + 1 - core]
    sub = lax.broadcasted_iota(jnp.int32, (8, LANES), 0)
    lane = lax.broadcasted_iota(jnp.int32, (8, LANES), 1)
    last = jnp.zeros((8, LANES), jnp.int32)
    for slot, block in enumerate(block_of):
        last = jnp.where(sub == slot, (block + 1) * rows - 1, last)
    mine = me * rows + sub * LANES + lane

    def scan(c, carry):
        end, begin_last, end_last, begin_mine, end_mine = carry
        end = end + sizes_ref[c]
        done = end <= last
        begin_last = jnp.where(done, end, begin_last)
        end_last = jnp.where(done, end_last, jnp.minimum(end_last, end))
        done = end <= mine
        begin_mine = jnp.where(done, end, begin_mine)
        end_mine = jnp.where(done, end_mine, jnp.minimum(end_mine, end))
        return end, begin_last, end_last, begin_mine, end_mine

    zero = jnp.zeros((8, LANES), jnp.int32)
    top = jnp.full((8, LANES), 1 << 30, jnp.int32)
    carry = (jnp.int32(0), zero, top, zero, top)
    carry = lax.fori_loop(0, clusters, scan, carry, unroll=8)
    _, begin_last, end_last, begin_mine, end_mine = carry
    low = [begin_last[s:s + 1] for s in range(5)]
    high = [end_last[s:s + 1] for s in range(5)]
    lane_row = lax.broadcasted_iota(jnp.int32, (1, LANES), 1)

    def index_row(slot, t):
        return block_of[slot] * rows + t * LANES + lane_row

    def clipped(slot):
        return jnp.clip(block_of[slot], 0, devices - 1)

    def rank_row(slot, t):
        return order_ref[pl.ds(clipped(slot) * tiles + t, 1), :].astype(jnp.float32)

    def spread(row):
        return jnp.transpose(jnp.broadcast_to(row, (LANES, LANES)))

    for slot in range(5):
        for t in range(tiles):
            row = jnp.where(index_row(slot, t) >= low[slot], rank_row(slot, t), BIG)
            col[slot, pl.ds(t * LANES, LANES), :] = spread(row)
    for t in range(tiles):
        col[5, pl.ds(t * LANES, LANES), :] = spread(rank_row(OWN, t))
    acc_low[...] = jnp.full(acc_low.shape, -1.0, jnp.float32)
    acc_high[...] = jnp.full(acc_high.shape, -1.0, jnp.float32)

    pl.semaphore_wait(barrier, 3 + has_down.astype(jnp.int32) + has_up.astype(jnp.int32))

    load.wait()

    def chunk(c):
        return pl.ds(c * piece, piece)

    def own_copy(slot, c, target):
        return pltpu.make_async_remote_copy(
            src_ref=raw.at[OWN, chunk(c)], dst_ref=raw.at[slot, chunk(c)],
            send_sem=send_sem.at[slot, c], recv_sem=recv_sem.at[slot, c],
            device_id=dev(target), device_id_type=MESH)

    def far_copy(c):
        return pltpu.make_async_remote_copy(
            src_ref=raw.at[WHY, chunk(c)], dst_ref=raw.at[FAR, chunk(c)],
            send_sem=send_sem.at[FAR, c], recv_sem=recv_sem.at[FAR, c],
            device_id=dev(partner), device_id_type=MESH)

    def part_copy():
        return pltpu.make_async_remote_copy(
            src_ref=raw.at[OWN], dst_ref=raw.at[PART],
            send_sem=send_sem.at[PART, 0], recv_sem=recv_sem.at[PART, 0],
            device_id=dev(partner), device_id_type=MESH)

    def ret_copy(slot, target):
        return pltpu.make_async_remote_copy(
            src_ref=back.at[slot], dst_ref=ret.at[slot],
            send_sem=ret_send.at[slot], recv_sem=ret_recv.at[slot],
            device_id=dev(target), device_id_type=MESH)

    z_target = jnp.where(on_b, me + 4, me - 4)
    sends_z = jnp.where(on_b, has_up, has_down)
    takes_z = jnp.where(on_b, has_down, has_up)
    sends_part = core == is_a
    takes_part = core == is_b
    sent = []

    @pl.when(on_a)
    def _():
        for c in range(CHUNKS):
            own_copy(WHY, c, me + 2).start()

    @pl.when(sends_z)
    def _():
        for c in range(CHUNKS):
            own_copy(ZED, c, z_target).start()

    @pl.when(sends_part)
    def _():
        part_copy().start()

    def normalize(slot, start, count):
        at = pl.ds(start, count)
        values = raw[slot, at, :].astype(jnp.float32)
        total = jnp.sum(values * values, axis=1, keepdims=True)
        unit[slot, at, :] = (values * lax.rsqrt(total + 1e-06)).astype(jnp.bfloat16)

    def dot(a, b):
        return lax.dot_general(a, b, (((1,), (1,)), ((), ())), preferred_element_type=jnp.float32)

    def fold(x):
        return jnp.max(x.reshape(x.shape[0] // 8, 8, x.shape[1]), axis=0)

    def pair(lower, start, count, higher, first_col, cols):
        others = unit[higher, pl.ds(first_col, cols), :]
        ranks, inside = [], []
        for t in range(first_col // LANES, (first_col + cols) // LANES):
            within = index_row(higher, t) < high[lower]
            inside.append(within)
            ranks.append(jnp.where(within, rank_row(higher, t), 2 * BIG))

        def step(i, carry):
            at = pl.ds(pl.multiple_of(start + i * LANES, LANES), LANES)
            scores = dot(unit[lower, at, :], others)
            ranks_low = col[lower, at, :]
            best = acc_low[lower, at, :]
            result = []
            for n in range(len(ranks)):
                s = scores[:, n * LANES:(n + 1) * LANES]
                before = ranks_low < ranks[n]
                best = jnp.maximum(best, jnp.where(before, -1.0, s))
                result.append(jnp.maximum(carry[n], fold(jnp.where(before, s, -1.0))))
            acc_low[lower, at, :] = best
            return tuple(result)

        found = tuple(jnp.full((8, LANES), -1.0, jnp.float32) for _ in ranks)
        found = lax.fori_loop(0, count // LANES, step, found)
        for n in range(len(ranks)):
            at = pl.ds(first_col + n * LANES, LANES)
            masked = jnp.where(inside[n], found[n], -1.0)
            acc_high[higher, :, at] = jnp.maximum(acc_high[higher, :, at], masked)

    def within_own():
        others = unit[OWN]
        ranks = [rank_row(OWN, t) for t in range(tiles)]
        begins = [begin_mine[t:t + 1] for t in range(tiles)]
        ends = [end_mine[t:t + 1] for t in range(tiles)]

        def step(i, carry):
            at = pl.ds(pl.multiple_of(i * LANES, LANES), LANES)
            scores = dot(unit[OWN, at, :], others)
            ranks_low = col[5, at, :]
            index = me * rows + i * LANES + lax.broadcasted_iota(jnp.int32, (LANES, LANES), 0)
            result = []
            for n in range(tiles):
                s = scores[:, n * LANES:(n + 1) * LANES]
                keep = (ranks_low < ranks[n]) & (index >= begins[n]) & (index < ends[n])
                result.append(jnp.maximum(carry[n], fold(jnp.where(keep, s, -1.0))))
            return tuple(result)

        found = tuple(jnp.full((8, LANES), -1.0, jnp.float32) for _ in ranks)
        found = lax.fori_loop(0, tiles, step, found)
        for n in range(tiles):
            at = pl.ds(n * LANES, LANES)
            acc_high[OWN, :, at] = jnp.maximum(acc_high[OWN, :, at], found[n])

    def result_of(slot, lows=True):
        pieces = []
        for t in range(tiles):
            at = pl.ds(t * LANES, LANES)
            best = jnp.max(acc_high[slot, :, at], axis=0, keepdims=True)
            if lows:
                found = jnp.max(jnp.transpose(acc_low[slot, at, :]), axis=0, keepdims=True)
                best = jnp.maximum(best, jnp.where(index_row(slot, t) >= low[slot], found, -1.0))
            pieces.append(best)
        return jnp.concatenate(pieces, axis=1)

    normalize(OWN, 0, rows)
    within_own()

    @pl.when(takes_part)
    def _():
        part_copy().wait_recv()
        normalize(PART, 0, rows)

    @pl.when(both(on_b, second))
    def _():
        pair(PART, 0, rows, OWN, 0, rows)

    @pl.when(both(on_a, first))
    def _():
        pair(OWN, 0, rows, PART, 0, rows)

    @pl.when(on_b)
    def _():
        for c in range(CHUNKS):
            start = c * piece
            own_copy(WHY, c, partner).wait_recv()
            far_copy(c).start()
            normalize(WHY, start, piece)
            pair(WHY, start, piece, OWN, 0, rows)

            @pl.when(has_down)
            def _():
                own_copy(ZED, c, partner).wait_recv()
                normalize(ZED, start, piece)
                pair(ZED, start, piece, OWN, 0, rows)

                @pl.when(second)
                def _():
                    pair(ZED, start, piece, PART, 0, rows)

                pair(ZED, start, piece, WHY, 0, start + piece)
                if c:
                    pair(ZED, 0, start, WHY, start, piece)

            if c == CHUNKS - 1:
                back[2] = result_of(WHY)

                @pl.when(first)
                def _():
                    ret_copy(2, me - 2).start()

                @pl.when(second)
                def _():
                    pltpu.make_async_remote_copy(
                        src_ref=back.at[2], dst_ref=ret.at[3], send_sem=ret_send.at[2],
                        recv_sem=ret_recv.at[3], device_id=dev(me - 2), device_id_type=MESH).start()
                    back[1] = result_of(PART)
                    ret_copy(1, partner).start()

            far_copy(c).wait_recv()
            normalize(FAR, start, piece)
            pair(FAR, start, piece, OWN, 0, rows)

            @pl.when(has_down)
            def _():
                pair(ZED, start, piece, FAR, 0, start + piece)
                if c:
                    pair(ZED, 0, start, FAR, start, piece)

        back[3] = result_of(FAR)

        @pl.when(first)
        def _():
            pltpu.make_async_remote_copy(
                src_ref=back.at[3], dst_ref=ret.at[2], send_sem=ret_send.at[3], recv_sem=ret_recv.at[2],
                device_id=dev(me - 1), device_id_type=MESH).start()

        @pl.when(second)
        def _():
            ret_copy(3, me - 3).start()

        @pl.when(has_down)
        def _():
            back[0] = result_of(ZED)
            ret_copy(0, me - 4).start()

    @pl.when(on_a)
    def _():
        @pl.when(has_up)
        def _():
            for c in range(CHUNKS):
                start = c * piece
                own_copy(ZED, c, partner).wait_recv()
                normalize(ZED, start, piece)
                pair(OWN, 0, rows, ZED, start, piece)

                @pl.when(first)
                def _():
                    pair(PART, 0, rows, ZED, start, piece)

            back[0] = result_of(ZED, False)
            ret_copy(0, me + 4).start()

        @pl.when(first)
        def _():
            back[1] = result_of(PART)
            ret_copy(1, partner).start()

    out_ref[...] = result_of(OWN)

    def take(slot):
        ret_copy(slot, partner).wait_recv()
        out_ref[...] = jnp.maximum(out_ref[...], ret[slot])

    pl.when(sends_part)(lambda: take(1))
    pl.when(sends_z)(lambda: take(0))

    @pl.when(on_a)
    def _():
        take(2)
        take(3)

    for c in range(CHUNKS):
        pl.when(sends_z)(lambda: own_copy(ZED, c, partner).wait_send())
        pl.when(on_a)(lambda: own_copy(WHY, c, partner).wait_send())
        pl.when(on_b)(lambda: far_copy(c).wait_send())
    pl.when(sends_part)(lambda: part_copy().wait_send())
    pl.when(takes_part)(lambda: ret_copy(1, partner).wait_send())
    pl.when(takes_z)(lambda: ret_copy(0, partner).wait_send())

    @pl.when(on_b)
    def _():
        ret_copy(2, partner).wait_send()
        ret_copy(3, partner).wait_send()


def local(embeddings, sizes, order, devices):
    rows, width = embeddings.shape
    order = order.reshape(-1, LANES)
    result = pl.pallas_call(
        functools.partial(kernel, devices),
        out_shape=pltpu.VMEM((1, rows), jnp.float32),
        in_specs=[
            pl.BlockSpec(memory_space=pl.ANY),
            pl.BlockSpec(memory_space=pl.ANY),
            pl.BlockSpec(memory_space=pl.ANY),
        ],
        out_specs=pl.BlockSpec(memory_space=pltpu.VMEM),
        scratch_shapes=[
            pltpu.SMEM(sizes.shape, jnp.int32),
            pltpu.VMEM(order.shape, jnp.int32),
            pltpu.VMEM((5, rows, width), jnp.bfloat16),
            pltpu.VMEM((5, rows, width), jnp.bfloat16),
            pltpu.VMEM((6, rows, LANES), jnp.float32),
            pltpu.VMEM((5, rows, LANES), jnp.float32),
            pltpu.VMEM((5, 8, rows), jnp.float32),
            pltpu.VMEM((4, 1, rows), jnp.float32),
            pltpu.VMEM((4, 1, rows), jnp.float32),
            pltpu.SemaphoreType.DMA,
            pltpu.SemaphoreType.DMA((2,)),
            pltpu.SemaphoreType.DMA((5, CHUNKS)),
            pltpu.SemaphoreType.DMA((5, CHUNKS)),
            pltpu.SemaphoreType.DMA((4,)),
            pltpu.SemaphoreType.DMA((4,)),
        ],
        compiler_params=pltpu.CompilerParams(collective_id=0, has_side_effects=True),
    )(embeddings, sizes, order)
    return result.reshape(rows)


def solution(mesh):
    return jax.shard_map(
        functools.partial(local, devices=mesh.shape["row"]),
        mesh=mesh,
        in_specs=(P(("parts", "row"), None), P("parts"), P("parts")),
        out_specs=P(("parts", "row")),
        check_vma=False,
    )
```
